512 devices in a mesh: grp: 2 (over z_hi), gz: 32 (over z_lo, y), xy: 8 (over x, core).
Axes of the slice: x: 4, y: 4, z: 16 (z_hi: 2, z_lo: 8; z = z_hi * 8 + z_lo), core: 2. Of those that a mesh axis runs over, the one named last changes fastest.
Arguments:
- velocity: float32 [2, 3, 32, 512, 512], P('grp', None, 'gz', 'xy'), may hold values from -6 to 6
- fringe_columns: int32 [128], replicated, may hold values from 0 to 511, as said below
Outputs:
- velocity_next: float32 [2, 3, 32, 512, 512], P('grp', None, 'gz', 'xy')
The draws below stay inside these ranges and needn't reach their ends.
Inputs may be any that keep to these rules, and one draw needn't show every extreme that they name: `fringe_columns`: 128 consecutive precursor columns, counted modulo 512, from a start that varies; the run always passes column 511 and wraps to column 0.
All inputs are finite; a program needn't handle non-finite values.
Results may differ from the reference program's by a relative error of at most 0.0001.
Values sent between devices are 32-bit elements; how exact they have to be, the bound alone decides.
No kernel may reach another device: no remote copies, remote signals or barrier semaphores. Data moves between devices by JAX's collectives and lax.ppermute only.
A program may use at most 64 MiB of HBM per device.

```python
import math
import jax
import jax.numpy as jnp
from jax import lax

NX = 512
NY = 512
STEPS = 2
NZ = 32
FRINGE = 128


def draw_fringe_columns(key, part):
    start_key = jax.random.fold_in(key, 7919)
    first = jax.random.randint(start_key, (), NX - FRINGE + 1, NX, dtype=jnp.int32)
    return ((first + jnp.arange(FRINGE, dtype=jnp.int32)) % NX).astype(jnp.int32)


def block_scale(own_key, dims, pieces, least, high):
    def one(axis_at, parts):
        steps = jax.random.uniform(jax.random.fold_in(jax.random.fold_in(own_key, 6), axis_at), (parts,), jnp.float32, least / len(pieces), high / len(pieces))
        return jnp.repeat(jnp.exp(steps), dims[axis_at] // parts).reshape((-1,) + (1,) * (len(dims) - axis_at - 1))

    gain = one(*pieces[0])
    for cut in pieces[1:]:
        gain = gain * one(*cut)
    return gain


def centred(own_key, dims, spread, bound, shards=(), kind=jnp.bfloat16):
    level = block_scale(own_key, dims, shards, -0.22, 0.18) if shards else 1.0
    entries = jax.random.normal(own_key, dims, jnp.float32) * spread * level
    return jnp.minimum(jnp.maximum(entries, -bound), bound).astype(kind)


def setup_inputs(seed: int = 0) -> dict:
    key_of = jax.random.split(jax.random.key(seed), 3)
    velocity = centred(key_of[0], (2, 3, NZ, NY, NX), 1.0, 6.0, ((0, 2), (2, 32), (3, 8)), jnp.float32)
    fringe_columns = draw_fringe_columns(jax.random.fold_in(key_of[2], 71), 0)
    return {"velocity": velocity, "fringe_columns": fringe_columns}


time_step = 0.001
level_gap = 0.05
smag_coeff = 0.16

def spectral_derivative(field, axis):
    moved = jnp.moveaxis(field, axis, -1)
    points = moved.shape[-1]
    wavenumber = jnp.arange(points // 2 + 1)
    wavenumber = jnp.where(wavenumber == points // 2, 0, wavenumber).astype(field.dtype)
    spectrum = jnp.fft.rfft(moved, axis=-1)
    result = jnp.fft.irfft(spectrum * (1j * wavenumber), n=points, axis=-1).astype(field.dtype)
    return jnp.moveaxis(result, -1, axis)

def vertical_derivative(field):
    padded = jnp.pad(field, ((0, 0), (1, 1), (0, 0), (0, 0)))
    return (padded[:, 2:] - padded[:, :-2]) / (2.0 * level_gap)

def tendency(velocity_now):
    along_x = spectral_derivative(velocity_now, 3)
    along_y = spectral_derivative(velocity_now, 2)
    along_z = vertical_derivative(velocity_now)
    gradient = jnp.stack([along_x, along_y, along_z], axis=1)
    strain = 0.5 * (gradient + jnp.swapaxes(gradient, 0, 1))
    delta = (2.0 * math.pi / NX * (2.0 * math.pi / NY) * level_gap) ** (1.0 / 3.0)
    eddy_visc = (smag_coeff * delta) ** 2 * jnp.sqrt(2.0 * lax.optimization_barrier(jnp.sum(strain * strain, axis=(0, 1))))
    stress = 2.0 * eddy_visc[None, None] * strain
    advection = lax.optimization_barrier(jnp.sum(gradient * velocity_now[None], axis=1))
    divergence = spectral_derivative(stress[:, 0], 3) + spectral_derivative(stress[:, 1], 2) + vertical_derivative(stress[:, 2])
    return divergence - advection

def reference(velocity, fringe_columns):
    farm_state = velocity[0]
    precursor = velocity[1]
    offsets = jnp.arange(FRINGE).astype(jnp.float32)
    weights = 0.5 * (1.0 + jnp.cos(jnp.pi * offsets / FRINGE))
    for step_index in range(STEPS):
        farm_state = farm_state + time_step * tendency(farm_state)
        precursor = precursor + time_step * tendency(precursor)
        picked = jnp.take(precursor, fringe_columns, axis=3)
        blended = (1.0 - weights) * farm_state[..., :FRINGE] + weights * picked
        farm_state = jnp.concatenate([blended, farm_state[..., FRINGE:]], axis=3)
    return jnp.stack([farm_state, precursor])
```

```python
import functools
import math

import jax
import jax.numpy as jnp
import numpy as np
from jax import lax
from jax.experimental import pallas as pl
from jax.experimental.pallas import tpu as pltpu
from jax.sharding import PartitionSpec as P

STEPS = 2

time_step = 0.001
level_gap = 0.05
smag_coeff = 0.16


def split_matrices(points):
    half = points // 2
    distance = np.arange(points)
    angle = np.pi * distance / points
    with np.errstate(divide="ignore", invalid="ignore"):
        row = 0.5 * (1.0 - 2.0 * (distance % 2)) * np.cos(angle) / np.sin(angle)
    row[0] = 0.0
    shift = np.arange(half)[None, :] - np.arange(half)[:, None]
    near = row[shift % points]
    far = row[(shift + half) % points]
    pieces = []
    for whole in (0.5 * (near + far), 0.5 * (near - far)):
        high = whole.astype(jnp.bfloat16)
        low = (whole - high.astype(np.float64)).astype(jnp.bfloat16)
        pieces += [high, low]
    return np.stack(pieces)


def product(left, high, low):
    left_high = left.astype(jnp.bfloat16)
    left_low = (left - left_high.astype(jnp.float32)).astype(jnp.bfloat16)
    dot = functools.partial(jnp.dot, preferred_element_type=jnp.float32)
    return dot(left_high, high) + (dot(left_low, high) + dot(left_high, low))


def derive(field, mats):
    half = field.shape[1] // 2
    first, second = field[:, :half], field[:, half:]
    even = product(first + second, mats[0], mats[1])
    odd = product(first - second, mats[2], mats[3])
    return jnp.concatenate([even + odd, even - odd], axis=1)


def row_pack(field, out, base):
    for p in range(2):
        lanes = [slice(256 * p + 128 * h, 256 * p + 128 * h + 128) for h in range(2)]
        parts = [field[0:128, lanes[0]].T, field[0:128, lanes[1]].T]
        parts.append(jnp.concatenate([field[128:192, lanes[0]], field[128:192, lanes[1]]], axis=0).T)
        for j in range(4):
            for n in range(3):
                out[4 * p + j, base + 32 * n : base + 32 * n + 32, :] = parts[n][32 * j : 32 * j + 32]


def row_unpack(got, base):
    top, bottom = [], []
    for p in range(2):
        parts = [
            jnp.concatenate(
                [got[4 * p + j, base + 32 * n : base + 32 * n + 32, :] for j in range(4)], axis=0
            ).T
            for n in range(3)
        ]
        top += parts[:2]
        bottom += [parts[2][0:64], parts[2][64:128]]
    return jnp.concatenate([jnp.concatenate(top, axis=1), jnp.concatenate(bottom, axis=1)], axis=0)


def swap_halves(one, two):
    left = lax.broadcasted_iota(jnp.int32, one.shape, 1) < 64
    return (
        jnp.where(left, one, pltpu.roll(two, 64, 1)),
        jnp.where(left, pltpu.roll(one, 64, 1), two),
    )


def col_unpack(load):
    tiles = []
    for m in range(4):
        low, high = swap_halves(load(2 * m), load(2 * m + 1))
        tiles.append(jnp.concatenate([low[0:64], high[0:64], low[64:96], high[64:96]], axis=0))
    return jnp.concatenate(tiles, axis=1)


def col_pack(field, out, base):
    for m in range(4):
        tile = field[:, 128 * m : 128 * m + 128]
        low = jnp.concatenate([tile[0:64], tile[128:160]], axis=0)
        high = jnp.concatenate([tile[64:128], tile[160:192]], axis=0)
        one, two = swap_halves(low, high)
        out[2 * m, base : base + 96, :] = one
        out[2 * m + 1, base : base + 96, :] = two


def strains(dx, dy, dz, delta):
    part = lambda a, i: a[64 * i : 64 * i + 64]
    xx, yy, zz = part(dx, 0), part(dy, 1), part(dz, 2)
    xy = 0.5 * (part(dx, 1) + part(dy, 0))
    xz = 0.5 * (part(dx, 2) + part(dz, 0))
    yz = 0.5 * (part(dy, 2) + part(dz, 1))
    total = xx * xx + yy * yy + zz * zz + 2.0 * (xy * xy + xz * xz + yz * yz)
    eddy = (smag_coeff * delta) ** 2 * jnp.sqrt(2.0 * total)
    return xx, yy, zz, xy, xz, yz, 2.0 * eddy


def pack_kernel(u, out):
    row_pack(u, out, 0)


def dx_kernel(u, mats, dx, out):
    along = derive(u[...], mats)
    dx[...] = along
    row_pack(along, out, 0)


def dy_kernel(got, packed, mats, dy, out):
    along = derive(col_unpack(lambda q: got[q]), mats)
    dy[...] = along
    out[:, 0:96, :] = packed[...]
    col_pack(along, out, 96)


def col_stress_kernel(delta, got, above, below, dy, mats, out):
    scale = 0.5 / level_gap
    dz = col_unpack(lambda q: (above[q] - below[q]) * scale)
    dx = col_unpack(lambda q: got[q, 0:96, :])
    xx, yy, zz, xy, xz, yz, twice = strains(dx, dy[...], dz, delta)
    stress = jnp.concatenate([twice * xy, twice * yy, twice * yz], axis=0)
    col_pack(derive(stress, mats), out, 0)


def row_stress_kernel(delta, u, above, below, got, dx, mats, part, stress_z):
    scale = 0.5 / level_gap
    dz = (above[...] - below[...]) * scale
    dy = row_unpack(got, 96)
    along = dx[...]
    xx, yy, zz, xy, xz, yz, twice = strains(along, dy, dz, delta)
    stress_z[...] = jnp.concatenate([twice * xz, twice * yz, twice * zz], axis=0)
    stress_x = jnp.concatenate([twice * xx, twice * xy, twice * xz], axis=0)
    now = u[...]
    u0, u1, u2 = (jnp.concatenate([now[64 * i : 64 * i + 64]] * 3, axis=0) for i in range(3))
    advection = u0 * along + u1 * dy + u2 * dz
    part[...] = now + time_step * (derive(stress_x, mats) - advection)


def update_kernel(start, part, above, below, got, new, picked):
    scale = 0.5 / level_gap
    new[...] = part[...] + time_step * (row_unpack(got, 0) + (above[...] - below[...]) * scale)
    first = start[0]
    tile, offset = first // 128, lax.rem(first, 128)
    one = new[:, pl.ds(pl.multiple_of(tile * 128, 128), 128)]
    two = new[:, pl.ds(pl.multiple_of(lax.rem(tile + 1, 4) * 128, 128), 128)]
    shift = lax.rem(128 - offset, 128)
    lane = lax.broadcasted_iota(jnp.int32, one.shape, 1)
    picked[...] = jnp.where(
        lane < 128 - offset, pltpu.roll(one, shift, 1), pltpu.roll(two, shift, 1)
    )


def blend(new, picked, weights):
    share = weights[...]
    return (1.0 - share) * new[:, 0:128] + share * picked[...]


def blend_pack_kernel(new, picked, weights, u, out):
    u[:, 0:128] = blend(new, picked, weights)
    u[:, 128:512] = new[:, 128:512]
    row_pack(u, out, 0)


def blend_kernel(new, picked, weights, u):
    u[:, 0:128] = blend(new, picked, weights)
    u[:, 128:512] = new[:, 128:512]


def call(kernel, shapes, *args, scalars=0):
    outs = [jax.ShapeDtypeStruct(s, jnp.float32) for s in shapes]
    vmem = pl.BlockSpec(memory_space=pltpu.VMEM)
    smem = pl.BlockSpec(memory_space=pltpu.SMEM)
    result = pl.pallas_call(
        kernel,
        out_shape=outs,
        in_specs=[smem] * scalars + [vmem] * (len(args) - scalars),
        out_specs=[vmem] * len(outs),
    )(*args)
    return result if len(outs) > 1 else result[0]


def exchange(blocks):
    return lax.all_to_all(blocks, "xy", 0, 0)


def neighbours(value):
    count = lax.axis_size("gz")
    above = lax.ppermute(value, "gz", [(i + 1, i) for i in range(count - 1)])
    below = lax.ppermute(value, "gz", [(i, i + 1) for i in range(count - 1)])
    return above, below


def per_device(velocity, fringe_columns):
    rows, columns = velocity.shape[3], velocity.shape[4]
    count = lax.axis_size("xy")
    delta = (2.0 * math.pi / columns * (2.0 * math.pi / (rows * count)) * level_gap) ** (1.0 / 3.0)
    mats = jnp.asarray(split_matrices(columns))
    width = fringe_columns.shape[0]
    weights = 0.5 * (1.0 + jnp.cos(jnp.pi * jnp.arange(width).astype(jnp.float32) / width))
    weights = jnp.where(lax.axis_index("grp") == 0, weights, 0.0).reshape(1, width)
    first = fringe_columns[0:1]

    whole, block = (3 * rows, columns), (count, 96, 128)
    pair = (count, 192, 128)
    u = velocity.reshape(whole)
    packed = call(pack_kernel, [block], u)
    for step_index in range(STEPS):
        columns_u = exchange(packed)
        above, below = neighbours(u)
        dx, dx_packed = call(dx_kernel, [whole, block], u, mats)
        dy_col, both = call(dy_kernel, [whole, pair], columns_u, dx_packed, mats)
        got = exchange(both)
        col_above, col_below = neighbours(columns_u)
        stress = call(
            functools.partial(col_stress_kernel, delta),
            [block], got, col_above, col_below, dy_col, mats,
        )
        back = exchange(stress)
        part, stress_z = call(
            functools.partial(row_stress_kernel, delta),
            [whole, whole], u, above, below, got, dx, mats,
        )
        z_above, z_below = neighbours(stress_z)
        new, picked = call(
            update_kernel, [whole, (3 * rows, width)], first, part, z_above, z_below, back, scalars=1
        )
        picked = lax.ppermute(picked, "grp", [(1, 0)])
        if step_index + 1 < STEPS:
            u, packed = call(blend_pack_kernel, [whole, block], new, picked, weights)
        else:
            u = call(blend_kernel, [whole], new, picked, weights)
    return u.reshape(velocity.shape)


def solution(mesh):
    in_specs = (P("grp", None, "gz", "xy", None), P())
    out_specs = P("grp", None, "gz", "xy", None)
    return jax.shard_map(
        per_device, mesh=mesh, in_specs=in_specs, out_specs=out_specs, check_vma=False
    )
```
